512 devices in a mesh: pb: 64 (over y_lo, x, z), ka: 8 (over y_hi, core).
Axes of the slice: x: 4, y: 8 (y_hi: 4, y_lo: 2; y = y_hi * 2 + y_lo), z: 8, core: 2. Of those that a mesh axis runs over, the one named last changes fastest.
Arguments:
- queries: bfloat16 [16384, 1024], P('pb'), may hold values from -40 to 40
- keys: bfloat16 [16384, 128], P(('ka', 'pb')), may hold values from -20 to 20
- values: bfloat16 [16384, 128], P(('ka', 'pb')), may hold values from -12 to 12
- dout: bfloat16 [16384, 1024], P('pb'), may hold values from -6 to 6
- block_mask: int32 [128, 128], P('pb', 'ka'), may hold values from 0 to 1, as said below
Outputs:
- attended: bfloat16 [16384, 1024], P('pb', 'ka')
- query_grad: float32 [16384, 1024], P('pb', 'ka')
- key_grad: float32 [16384, 128], P(('ka', 'pb'))
- value_grad: float32 [16384, 128], P(('ka', 'pb'))
The draws below stay inside these ranges and needn't reach their ends.
Inputs may be any that keep to these rules, and one draw needn't show every extreme that they name: block_mask[i, j] = 1 lets the 128 queries of block i see the 128 keys of block j. Rows 2 * i and 2 * i + 1 are equal; in both of them the entries of columns 2 * i and 2 * i + 1 are 1, and every aligned run of 16 columns holds at least one 1.
All inputs are finite; a program needn't handle non-finite values.
Results may differ from the reference program's by a relative error of at most 0.017.
Values may be sent and summed in bfloat16 or wider, within the bound.
No kernel may reach another device: no remote copies, remote signals or barrier semaphores. Data moves between devices by JAX's collectives and lax.ppermute only.
A program may use at most 64 MiB of HBM per device.

```python
import math
import jax
import jax.numpy as jnp
from jax import lax

HEADS = 8
HEAD_DIM = 128
BLOCK = 128
SEQ = 16384
NBLK = 128
N_KA = 8


def paired_fields(key):
    base_key = jax.random.fold_in(key, 7301)
    keys_q, keys_k, scale_q, scale_k = jax.random.split(base_key, 4)
    key_field = jnp.clip(jax.random.normal(keys_k, (SEQ, HEAD_DIM), jnp.float32), -6.0, 6.0)
    query_field = jnp.clip(jax.random.normal(keys_q, (SEQ, HEADS * HEAD_DIM), jnp.float32), -6.0, 6.0)
    key_field = key_field * jnp.exp(jax.random.uniform(scale_k, (SEQ, 1), jnp.float32, math.log(0.3), math.log(3.0)))
    query_field = query_field * jnp.exp(jax.random.uniform(scale_q, (SEQ, 1), jnp.float32, math.log(0.4), math.log(4.0)))
    return (query_field, key_field)


def draw_queries(key, part):
    return paired_fields(key)[0].astype(jnp.bfloat16)


def draw_keys(key, part):
    return paired_fields(key)[1].astype(jnp.bfloat16)


def draw_block_mask(key, part):
    count = SEQ // BLOCK
    pair_count = count // 2
    panel_blocks = count // N_KA
    roll_key, pick_key = jax.random.split(jax.random.fold_in(key, 4409))
    pair_ids = jnp.arange(pair_count, dtype=jnp.int32)[:, None]
    col_ids = jnp.arange(count, dtype=jnp.int32)[None, :]
    rolls = jax.random.randint(roll_key, (pair_count, count), 0, 100)
    chance = jnp.where(col_ids <= 2 * pair_ids + 1, 85, 15)
    picks = jax.random.randint(pick_key, (pair_count, N_KA), 0, panel_blocks)
    forced = col_ids % panel_blocks == picks[:, col_ids[0] // panel_blocks]
    live = (rolls < chance) | forced | (col_ids // 2 == pair_ids)
    return jnp.repeat(live.astype(jnp.int32), 2, axis=0)


def shard_levels(own_key, shape, cuts, smallest, top_value):
    level = 1.0
    for dim, parts in cuts:
        draws = jax.random.uniform(jax.random.fold_in(jax.random.fold_in(own_key, 6), dim), (parts,), jnp.float32, smallest / len(cuts), top_value / len(cuts))
        level = level * jnp.repeat(jnp.exp(draws), shape[dim] // parts).reshape((-1,) + (1,) * (len(shape) - 1 - dim))
    return level


def centred(key, dims, scale, reach, shards=(), kind=jnp.bfloat16):
    values = scale * jax.random.normal(key, dims, jnp.float32)
    if shards:
        values = values * shard_levels(key, dims, shards, -0.22, 0.18)
    return jnp.clip(values, -reach, reach).astype(kind)


def setup_inputs(seed: int = 0) -> dict:
    streams_of = jax.random.split(jax.random.key(seed), 6)
    queries = draw_queries(jax.random.fold_in(streams_of[5], 71), 0)
    keys = draw_keys(jax.random.fold_in(streams_of[5], 71), 0)
    values = centred(streams_of[2], (SEQ, HEAD_DIM), 2.0, 12.0, ((0, 512),))
    dout = centred(streams_of[3], (SEQ, HEADS * HEAD_DIM), 1.0, 6.0, ((0, 64),))
    block_mask = draw_block_mask(jax.random.fold_in(streams_of[5], 71), 0)
    return {"queries": queries, "keys": keys, "values": values, "dout": dout, "block_mask": block_mask}


def rounded(array_in):
    return lax.optimization_barrier(array_in.astype(jnp.bfloat16)).astype(jnp.float32)

def reference(queries, keys, values, dout, block_mask):
    score_scale = 1.0 / math.sqrt(HEAD_DIM)
    key_rows = SEQ // N_KA
    keys_wide = keys.astype(jnp.float32)
    values_wide = values.astype(jnp.float32)
    key_panels = keys_wide.reshape(N_KA, key_rows, HEAD_DIM)
    value_panels = values_wide.reshape(N_KA, key_rows, HEAD_DIM)
    query_blocks = queries.reshape(NBLK, BLOCK, HEADS, HEAD_DIM)
    dout_blocks = dout.reshape(NBLK, BLOCK, HEADS, HEAD_DIM)

    def one_block(carry, inputs):
        grad_key, grad_value = carry
        query_block, dout_block, mask_row = inputs
        query_wide = query_block.astype(jnp.float32)
        dout_wide = dout_block.astype(jnp.float32)
        live_keys = jnp.repeat(mask_row, BLOCK) > 0
        scores = jnp.einsum('qhd,kd->hqk', query_wide, keys_wide) * score_scale
        panel_scores = scores.reshape(HEADS, BLOCK, N_KA, key_rows)
        panel_live = live_keys.reshape(N_KA, key_rows)
        panel_max = lax.optimization_barrier(jnp.max(jnp.where(panel_live, panel_scores, -jnp.inf), axis=3))
        panel_weights = jnp.where(panel_live, jnp.exp(panel_scores - panel_max[..., None]), 0.0)
        panel_total = lax.optimization_barrier(jnp.sum(panel_weights, axis=3))
        panel_acc = jnp.einsum('hqnk,nkd->hqnd', rounded(panel_weights), value_panels)
        panel_out = rounded(panel_acc / panel_total[..., None])
        panel_lse = panel_max + jnp.log(panel_total)
        row_peak = lax.optimization_barrier(jnp.max(panel_lse, axis=2))
        row_lse = row_peak + jnp.log(lax.optimization_barrier(jnp.sum(jnp.exp(panel_lse - row_peak[..., None]), axis=2)))
        mixing = jnp.exp(panel_lse - row_lse[..., None])
        attended = lax.optimization_barrier(jnp.sum(mixing[..., None] * panel_out, axis=2)).astype(jnp.bfloat16)
        row_delta = lax.optimization_barrier(jnp.sum(dout_wide.transpose(1, 0, 2) * attended.astype(jnp.float32), axis=2))
        probs = jnp.where(live_keys, jnp.exp(scores - row_lse[..., None]), 0.0)
        probs_low = rounded(probs)
        grad_value = grad_value + jnp.einsum('hqk,qhd->kd', probs_low, dout_wide)
        dprobs = jnp.einsum('qhd,kd->hqk', dout_wide, values_wide)
        dscores = rounded(probs * (dprobs - row_delta[..., None]))
        panel_dq = rounded(jnp.einsum('hqnk,nkd->qhnd', dscores.reshape(HEADS, BLOCK, N_KA, key_rows), key_panels) * score_scale)
        grad_query = lax.optimization_barrier(jnp.sum(panel_dq, axis=2))
        grad_key = grad_key + jnp.einsum('hqk,qhd->kd', dscores, query_wide) * score_scale
        out_rows = attended.transpose(1, 0, 2).reshape(BLOCK, HEADS * HEAD_DIM)
        return ((grad_key, grad_value), (out_rows, grad_query.reshape(BLOCK, HEADS * HEAD_DIM)))
    start = (jnp.zeros((SEQ, HEAD_DIM), jnp.float32), jnp.zeros((SEQ, HEAD_DIM), jnp.float32))
    (grad_key, grad_value), (attended, grad_query) = lax.scan(one_block, start, (query_blocks, dout_blocks, block_mask))
    return (attended.reshape(SEQ, HEADS * HEAD_DIM), grad_query.reshape(SEQ, HEADS * HEAD_DIM), grad_key, grad_value)
```

```python
import math

import jax
import jax.numpy as jnp
from jax import lax
from jax.experimental import pallas as pl
from jax.experimental.pallas import tpu as pltpu
from jax.sharding import PartitionSpec as P

BLOCK = 128
CHUNK = 256
DEAD = 1.0e30
F32 = jnp.float32
BF16 = jnp.bfloat16


def nt_dot(a, b):
    return lax.dot_general(a, b, (((1,), (1,)), ((), ())), preferred_element_type=F32)


def identity(size):
    rows = lax.broadcasted_iota(jnp.int32, (size, size), 0)
    cols = lax.broadcasted_iota(jnp.int32, (size, size), 1)
    return (rows == cols).astype(F32).astype(BF16)


def forward_kernel(
    mask_ref, kv_ref, q_ref, dout_ref, weights_ref, out_ref, stats_ref, peak_ref, scores, values_t
):
    keys, width = kv_ref.shape[0], kv_ref.shape[1] // 2
    queries, heads = q_ref.shape[0], q_ref.shape[1] // width
    scale = math.log2(math.e) / math.sqrt(width)
    eye = identity(width)
    values_t[...] = nt_dot(eye, kv_ref[:, width:]).astype(BF16)

    def one_head(h, carry):
        cols = pl.ds(pl.multiple_of(h * width, width), width)
        lanes = pl.ds(pl.multiple_of(h * queries, queries), queries)
        query = q_ref[:, cols]
        tops = []
        for start in range(0, keys, CHUNK):
            block = nt_dot(kv_ref[start : start + CHUNK, :width], query) * scale
            scores[start : start + CHUNK, :] = block
            for part in range(0, CHUNK, BLOCK):
                dead = jnp.where(mask_ref[0, (start + part) // BLOCK] > 0, 0.0, DEAD)
                top = jnp.max(block[part : part + BLOCK], axis=0, keepdims=True)
                tops.append((top - dead, dead))
        peak = tops[0][0]
        for top, _ in tops[1:]:
            peak = jnp.maximum(peak, top)
        total = jnp.zeros((1, queries), F32)
        for index, (_, dead) in enumerate(tops):
            start = index * BLOCK
            block = jnp.exp2(scores[start : start + BLOCK, :] - (peak + dead))
            weights_ref[start : start + BLOCK, lanes] = block.astype(BF16)
            total = total + jnp.sum(block, axis=0, keepdims=True)
        acc = jnp.dot(values_t[...], weights_ref[:, lanes], preferred_element_type=F32)
        out = acc / total
        delta = jnp.sum(nt_dot(eye, dout_ref[:, cols]) * out, axis=0, keepdims=True)
        out_ref[h] = out.astype(BF16)
        stats_ref[pl.ds(h, 1), :] = peak + jnp.log2(total)
        stats_ref[pl.ds(heads + h, 1), :] = delta
        peak_ref[pl.ds(h, 1), :] = peak
        return carry

    lax.fori_loop(0, heads, one_head, 0)


def row_mix(stats_ref, heads):
    panels = stats_ref.shape[0]
    top = stats_ref[0, :heads]
    for n in range(1, panels):
        top = jnp.maximum(top, stats_ref[n, :heads])
    total = jnp.zeros_like(top)
    delta = jnp.zeros_like(top)
    for n in range(panels):
        share = jnp.exp2(stats_ref[n, :heads] - top)
        total = total + share
        delta = delta + share * stats_ref[n, heads:]
    return top + jnp.log2(total), delta / total


def backward_kernel(
    stats_ref, peak_ref, kv_ref, q_ref, dout_ref, weights_ref, dq_ref, dkv_ref,
    dscores, keys_t, mixed_q, mixed_dout, factors,
):
    keys, width = kv_ref.shape[0], kv_ref.shape[1] // 2
    queries, heads = q_ref.shape[0], q_ref.shape[1] // width
    scale = 1.0 / math.sqrt(width)
    keys_t[...] = nt_dot(identity(width), kv_ref[:, :width]).astype(BF16)
    row_lse, row_delta = row_mix(stats_ref, heads)
    factor = jnp.exp2(peak_ref[...] - row_lse)
    factors[:heads, :] = factor
    factors[heads:, :] = row_delta
    columns = factor.T
    for h in range(heads):
        rows = slice(h * queries, (h + 1) * queries)
        cols = slice(h * width, (h + 1) * width)
        column = columns[:, h : h + 1]
        mixed_q[rows, :] = (q_ref[:, cols].astype(F32) * column).astype(BF16)
        mixed_dout[rows, :] = (dout_ref[:, cols].astype(F32) * column).astype(BF16)

    def one_head(h, carry):
        cols = pl.ds(pl.multiple_of(h * width, width), width)
        lanes = pl.ds(pl.multiple_of(h * queries, queries), queries)
        cotangent = dout_ref[:, cols]
        delta = factors[pl.ds(heads + h, 1), :]
        for start in range(0, keys, CHUNK):
            rows = slice(start, start + CHUNK)
            dprobs = nt_dot(kv_ref[rows, width:], cotangent)
            dscores[rows, lanes] = (weights_ref[rows, lanes].astype(F32) * (dprobs - delta)).astype(
                BF16
            )
        acc = jnp.dot(keys_t[...], dscores[:, lanes], preferred_element_type=F32)
        dq_ref[h] = (acc * (factors[pl.ds(h, 1), :] * scale)).astype(BF16)
        return carry

    lax.fori_loop(0, heads, one_head, 0)

    def one_chunk(index, carry):
        rows = pl.ds(pl.multiple_of(index * CHUNK, CHUNK), CHUNK)
        key_part = jnp.dot(dscores[rows, :], mixed_q[...], preferred_element_type=F32)
        value_part = jnp.dot(weights_ref[rows, :], mixed_dout[...], preferred_element_type=F32)
        dkv_ref[rows, :width] = (key_part * scale).astype(BF16)
        dkv_ref[rows, width:] = value_part.astype(BF16)
        return carry

    lax.fori_loop(0, keys // CHUNK, one_chunk, 0)


def attended_kernel(own_ref, stats_ref, parts_ref, attended_ref):
    panels, heads = parts_ref.shape[0], stats_ref.shape[1] // 2
    own = own_ref[0]
    row_lse, _ = row_mix(stats_ref, heads)
    picked = lax.broadcasted_iota(jnp.int32, row_lse.shape, 0) == own
    total = jnp.zeros(parts_ref.shape[1:], F32)
    for n in range(panels):
        mixing = jnp.exp2(stats_ref[n, :heads] - row_lse)
        mixing = jnp.sum(jnp.where(picked, mixing, 0.0), axis=0, keepdims=True)
        total = total + parts_ref[n].astype(F32) * mixing
    attended_ref[...] = total.T.astype(BF16)


def finish_kernel(dq_ref, dkv_ref, query_grad_ref, key_grad_ref, value_grad_ref):
    width = key_grad_ref.shape[1]
    total = dq_ref[0].astype(F32)
    for n in range(1, dq_ref.shape[0]):
        total = total + dq_ref[n].astype(F32)
    query_grad_ref[...] = total.T
    both = dkv_ref[0].astype(F32)
    for n in range(1, dkv_ref.shape[0]):
        both = both + dkv_ref[n].astype(F32)
    key_grad_ref[...] = both[:, :width]
    value_grad_ref[...] = both[:, width:]


VMEM = pl.BlockSpec(memory_space=pltpu.VMEM)
SMEM = pl.BlockSpec(memory_space=pltpu.SMEM)


def per_device(queries, keys, values, dout, block_mask):
    rows, row_width = queries.shape
    shard, width = keys.shape
    heads = row_width // width
    pb, ka = lax.axis_size("pb"), lax.axis_size("ka")
    panel = shard * pb
    all_rows = heads * rows
    shape = jax.ShapeDtypeStruct

    both = jnp.concatenate([keys, values], axis=1)
    copies = jnp.broadcast_to(both[None], (pb, shard, 2 * width))
    kv = lax.all_to_all(copies, "pb", 0, 0, tiled=True).reshape(panel, 2 * width)

    weights, out_parts, stats, peak = pl.pallas_call(
        forward_kernel,
        out_shape=(
            shape((panel, all_rows), BF16),
            shape((heads, width, rows), BF16),
            shape((2 * heads, rows), F32),
            shape((heads, rows), F32),
        ),
        in_specs=[SMEM, VMEM, VMEM, VMEM],
        out_specs=(VMEM,) * 4,
        scratch_shapes=[pltpu.VMEM((panel, rows), F32), pltpu.VMEM((width, panel), BF16)],
        name="forward",
    )(block_mask, kv, queries, dout)

    all_stats = lax.all_gather(stats, "ka")
    parts = lax.all_to_all(out_parts, "ka", 0, 0, tiled=True)

    dq_parts, dkv = pl.pallas_call(
        backward_kernel,
        out_shape=(shape((heads, width, rows), BF16), shape((panel, 2 * width), BF16)),
        in_specs=[VMEM] * 6,
        out_specs=(VMEM,) * 2,
        scratch_shapes=[
            pltpu.VMEM((panel, all_rows), BF16),
            pltpu.VMEM((width, panel), BF16),
            pltpu.VMEM((all_rows, width), BF16),
            pltpu.VMEM((all_rows, width), BF16),
            pltpu.VMEM((2 * heads, rows), F32),
        ],
        name="backward",
    )(all_stats, peak, kv, queries, dout, weights)

    own = lax.axis_index("ka").astype(jnp.int32).reshape(1)
    attended = pl.pallas_call(
        attended_kernel,
        out_shape=shape((rows, width), BF16),
        in_specs=[SMEM, VMEM, VMEM],
        out_specs=VMEM,
        name="attended",
    )(own, all_stats, parts)

    dq_own = lax.all_to_all(dq_parts, "ka", 0, 0, tiled=True)
    dkv_own = lax.all_to_all(dkv.reshape(pb, shard, 2 * width), "pb", 0, 0, tiled=True)
    query_grad, key_grad, value_grad = pl.pallas_call(
        finish_kernel,
        out_shape=(shape((rows, width), F32), shape((shard, width), F32), shape((shard, width), F32)),
        in_specs=[VMEM, VMEM],
        out_specs=(VMEM,) * 3,
        name="finish",
    )(dq_own, dkv_own)
    return attended, query_grad, key_grad, value_grad


def solution(mesh):
    in_specs = (
        P("pb", None),
        P(("ka", "pb"), None),
        P(("ka", "pb"), None),
        P("pb", None),
        P("pb", "ka"),
    )
    out_specs = (P("pb", "ka"), P("pb", "ka"), P(("ka", "pb"), None), P(("ka", "pb"), None))
    return jax.shard_map(
        per_device, mesh=mesh, in_specs=in_specs, out_specs=out_specs, check_vma=False
    )
```

```python
import math

import jax
import jax.numpy as jnp
from jax import lax
from jax.experimental import pallas as pl
from jax.experimental.pallas import tpu as pltpu
from jax.sharding import Mesh, PartitionSpec as P


BLOCK = 128
CHUNK = 512
SCORE_ROWS = 1024
GRAD_ROWS = 1024
DEAD = 1.0e30
F32 = jnp.float32
BF16 = jnp.bfloat16


def nt_dot(a, b):
    return lax.dot_general(a, b, (((1,), (1,)), ((), ())), preferred_element_type=F32)


def identity(size):
    rows = lax.broadcasted_iota(jnp.int32, (size, size), 0)
    cols = lax.broadcasted_iota(jnp.int32, (size, size), 1)
    return (rows == cols).astype(F32).astype(BF16)


def prepare_kernel(mask_ref, q_ref, dout_ref, q_out, dout_out, dead_ref):
    q_out[...] = q_ref[...]
    dout_out[...] = dout_ref[...]
    for j in range(dead_ref.shape[0]):
        dead = jnp.where(mask_ref[0, j] > 0, 0.0, DEAD)
        dead_ref[j : j + 1, :] = jnp.full((1, dead_ref.shape[1]), dead, F32)


def forward_kernel(
    dead_ref, kv_ref, q_ref, dout_ref, weights_ref, out_ref, stats_ref, peak_ref,
    scores_a, scores_b, wide,
):
    keys, width = kv_ref.shape[0], kv_ref.shape[1] // 2
    queries, heads = q_ref.shape[0], q_ref.shape[1] // width
    scale = 1.0 / math.sqrt(width)
    eye = identity(width)
    wide[width:, :] = jnp.ones((wide.shape[0] - width, keys), BF16)
    for start in range(0, keys, CHUNK):
        rows = slice(start, start + CHUNK)
        wide[:width, rows] = nt_dot(eye, kv_ref[rows, width:]).astype(BF16)
    scores = (scores_a, scores_b)
    tops = {}

    def score(h, start):
        query = q_ref[:, h * width : (h + 1) * width]
        block = nt_dot(kv_ref[start : start + SCORE_ROWS, :width], query) * scale
        scores[h % 2][start : start + SCORE_ROWS, :] = block
        for part in range(0, SCORE_ROWS, BLOCK):
            top = jnp.max(block[part : part + BLOCK].reshape(BLOCK // 8, 8, queries), axis=0)
            block_index = (start + part) // BLOCK
            top = top - dead_ref[block_index : block_index + 1, :]
            tops[h] = jnp.maximum(tops[h], top) if h in tops else top

    def weigh(h, j, peak):
        rows = slice(j * BLOCK, (j + 1) * BLOCK)
        block = jnp.exp(scores[h % 2][rows, :] - (peak + dead_ref[j : j + 1, :]))
        weights_ref[rows, h * queries : (h + 1) * queries] = block.astype(BF16)

    def combine(h, peak):
        lanes = slice(h * queries, (h + 1) * queries)
        acc = jnp.dot(wide[...], weights_ref[:, lanes], preferred_element_type=F32)
        total = acc[width : width + 1]
        out = acc[:width] / total
        out_ref[h] = out.astype(BF16)
        cotangent = nt_dot(eye, dout_ref[:, h * width : (h + 1) * width])
        stats_ref[h : h + 1, :] = peak + jnp.log(total)
        stats_ref[heads + h : heads + h + 1, :] = jnp.sum(cotangent * out, axis=0, keepdims=True)
        peak_ref[h : h + 1, :] = peak

    for start in range(0, keys, SCORE_ROWS):
        score(0, start)
    before = None
    for h in range(heads):
        peak = jnp.max(tops[h], axis=0, keepdims=True)
        for start in range(0, keys, SCORE_ROWS):
            if h + 1 < heads:
                score(h + 1, start)
            for j in range(start // BLOCK, (start + SCORE_ROWS) // BLOCK):
                weigh(h, j, peak)
        if before is not None:
            combine(h - 1, before)
        before = peak
    combine(heads - 1, before)


def row_mix(stats_ref, heads):
    panels = stats_ref.shape[0]
    top = stats_ref[0, :heads]
    for n in range(1, panels):
        top = jnp.maximum(top, stats_ref[n, :heads])
    total = jnp.zeros_like(top)
    delta = jnp.zeros_like(top)
    for n in range(panels):
        share = jnp.exp(stats_ref[n, :heads] - top)
        total = total + share
        delta = delta + share * stats_ref[n, heads:]
    return top + jnp.log(total), delta / total


def backward_kernel(
    stats_ref, peak_ref, own_ref, kv_ref, q_ref, dout_ref, weights_ref, out_ref,
    keep_ref, send_ref, dkv_ref, dscores, keys_t, mixed_q, mixed_dout, factors, blended,
):
    keys, width = kv_ref.shape[0], kv_ref.shape[1] // 2
    queries, heads = q_ref.shape[0], q_ref.shape[1] // width
    scale = 1.0 / math.sqrt(width)
    core = lax.axis_index("core")
    eye = identity(width)
    for start in range(0, keys, CHUNK):
        rows = slice(start, start + CHUNK)
        keys_t[:, rows] = nt_dot(eye, kv_ref[rows, :width]).astype(BF16)
    row_lse, row_delta = row_mix(stats_ref, heads)
    factor = jnp.exp(peak_ref[...] - row_lse)
    factors[:heads, :] = factor
    factors[heads : 2 * heads, :] = row_delta
    factors[2 * heads :, :] = jnp.exp(own_ref[:heads, :] - row_lse)
    columns = factor.T

    def mix(h):
        rows = slice(h * queries, (h + 1) * queries)
        cols = slice(h * width, (h + 1) * width)
        column = columns[:, h : h + 1]
        mixed_q[rows, :] = (q_ref[:, cols].astype(F32) * column).astype(BF16)
        mixed_dout[rows, :] = (dout_ref[:, cols].astype(F32) * column).astype(BF16)

    def differ(h, start):
        rows = slice(start, start + CHUNK)
        lanes = slice(h * queries, (h + 1) * queries)
        dprobs = nt_dot(kv_ref[rows, width:], dout_ref[:, h * width : (h + 1) * width])
        delta = factors[heads + h : heads + h + 1, :]
        dscores[rows, lanes] = (weights_ref[rows, lanes].astype(F32) * (dprobs - delta)).astype(BF16)

    def project(h):
        lanes = slice(h * queries, (h + 1) * queries)
        acc = jnp.dot(keys_t[...], dscores[:, lanes], preferred_element_type=F32)
        blended[h, :width, :] = (acc * (factors[h : h + 1, :] * scale)).astype(BF16)
        part = out_ref[h].astype(F32) * factors[2 * heads + h : 2 * heads + h + 1, :]
        blended[h, width:, :] = part.astype(BF16)

    for h in range(heads):
        for start in range(0, keys, CHUNK):
            differ(h, start)
        mix(h)
        if h:
            project(h - 1)
    project(heads - 1)

    def one_chunk(index, carry):
        rows = pl.ds(pl.multiple_of(index * GRAD_ROWS, GRAD_ROWS), GRAD_ROWS)
        key_part = jnp.dot(dscores[rows, :], mixed_q[...], preferred_element_type=F32)
        value_part = jnp.dot(weights_ref[rows, :], mixed_dout[...], preferred_element_type=F32)
        dkv_ref[rows, :width] = (key_part * scale).astype(BF16)
        dkv_ref[rows, width:] = value_part.astype(BF16)
        return carry

    lax.fori_loop(0, keys // GRAD_ROWS, one_chunk, 0)
    for index in range(heads // 2):
        keep_ref[index] = blended[2 * index + core]
        send_ref[index] = blended[2 * index + 1 - core]


def pair_kernel(keep_ref, got_ref, own_ref, one_ref, two_ref, three_ref):
    count = keep_ref.shape[0]
    place = lax.axis_index("y_hi")
    own_ref[...] = keep_ref[place].astype(F32) + got_ref[place].astype(F32)
    for step, target in enumerate((one_ref, two_ref, three_ref)):
        spot = lax.rem(place + step + 1, count)
        target[...] = (keep_ref[spot].astype(F32) + got_ref[spot].astype(F32)).astype(BF16)


def rows_kernel(own_ref, one_ref, two_ref, three_ref, query_grad_ref, attended_ref):
    width = query_grad_ref.shape[1]
    total = own_ref[...] + one_ref[...].astype(F32)
    total = total + two_ref[...].astype(F32) + three_ref[...].astype(F32)
    query_grad_ref[...] = total[:width].T
    attended_ref[...] = total[width:].T.astype(BF16)


def shards_kernel(parts_ref, key_grad_ref, value_grad_ref):
    width = key_grad_ref.shape[1]
    both = parts_ref[0].astype(F32)
    for n in range(1, parts_ref.shape[0]):
        both = both + parts_ref[n].astype(F32)
    key_grad_ref[...] = both[:, :width]
    value_grad_ref[...] = both[:, width:]


VMEM = pl.BlockSpec(memory_space=pltpu.VMEM)
SMEM = pl.BlockSpec(memory_space=pltpu.SMEM)


PB = ("y_lo", "x", "z")
KA = ("y_hi", "core")


def limit(mib):
    return pltpu.CompilerParams(vmem_limit_bytes=mib << 20)


def spread(block, axis):
    size = lax.axis_size(axis)
    copies = jnp.broadcast_to(block[None], (size,) + block.shape)
    return lax.all_to_all(copies, axis, 0, 0, tiled=True).reshape(-1, block.shape[1])


def per_device(queries, keys, values, dout, block_mask):
    rows, row_width = queries.shape
    shard, width = keys.shape
    heads = row_width // width
    pb, high = lax.axis_size(PB), lax.axis_size("y_hi")
    panel = shard * pb
    all_rows = heads * rows
    shape = jax.ShapeDtypeStruct

    kv = spread(jnp.concatenate([keys, values], axis=1), "z")
    kv = spread(kv, ("y_lo", "x"))

    q_near, dout_near, dead = pl.pallas_call(
        prepare_kernel,
        out_shape=(
            shape((rows, row_width), BF16),
            shape((rows, row_width), BF16),
            shape((panel // BLOCK, rows), F32),
        ),
        in_specs=[SMEM, VMEM, VMEM],
        out_specs=(VMEM,) * 3,
        compiler_params=limit(8),
        name="prepare",
    )(block_mask, queries, dout)

    weights, out_parts, stats, peak = pl.pallas_call(
        forward_kernel,
        out_shape=(
            shape((panel, all_rows), BF16),
            shape((heads, width, rows), BF16),
            shape((2 * heads, rows), F32),
            shape((heads, rows), F32),
        ),
        in_specs=[VMEM] * 4,
        out_specs=(VMEM,) * 4,
        scratch_shapes=[
            pltpu.VMEM((panel, rows), F32),
            pltpu.VMEM((panel, rows), F32),
            pltpu.VMEM((width + 16, panel), BF16),
        ],
        compiler_params=limit(20),
        name="forward",
    )(dead, kv, q_near, dout_near)

    all_stats = lax.all_gather(stats, KA)

    keep, send, dkv = pl.pallas_call(
        backward_kernel,
        out_shape=(
            shape((high, 2 * width, rows), BF16),
            shape((high, 2 * width, rows), BF16),
            shape((panel, 2 * width), BF16),
        ),
        in_specs=[VMEM] * 8,
        out_specs=(VMEM,) * 3,
        scratch_shapes=[
            pltpu.VMEM((panel, all_rows), BF16),
            pltpu.VMEM((width, panel), BF16),
            pltpu.VMEM((all_rows, width), BF16),
            pltpu.VMEM((all_rows, width), BF16),
            pltpu.VMEM((3 * heads, rows), F32),
            pltpu.VMEM((heads, 2 * width, rows), BF16),
        ],
        compiler_params=limit(30),
        name="backward",
    )(all_stats, peak, stats, kv, q_near, dout_near, weights, out_parts)

    dkv_own = lax.all_to_all(dkv.reshape(pb, shard, 2 * width), PB, 0, 0, tiled=True)
    got = lax.ppermute(send, "core", [(0, 1), (1, 0)])
    own, *moves = pl.pallas_call(
        pair_kernel,
        out_shape=(shape((2 * width, rows), F32),) + (shape((2 * width, rows), BF16),) * 3,
        in_specs=[VMEM, VMEM],
        out_specs=(VMEM,) * 4,
        compiler_params=limit(8),
        name="pair",
    )(keep, got)
    moved = [
        lax.ppermute(move, "y_hi", [(i, (i + step + 1) % high) for i in range(high)])
        for step, move in enumerate(moves)
    ]
    query_grad, attended = pl.pallas_call(
        rows_kernel,
        out_shape=(shape((rows, width), F32), shape((rows, width), BF16)),
        in_specs=[VMEM] * 4,
        out_specs=(VMEM,) * 2,
        compiler_params=limit(8),
        name="rows",
    )(own, *moved)
    key_grad, value_grad = pl.pallas_call(
        shards_kernel,
        out_shape=(shape((shard, width), F32), shape((shard, width), F32)),
        in_specs=[VMEM],
        out_specs=(VMEM,) * 2,
        compiler_params=limit(8),
        name="shards",
    )(dkv_own)
    return attended, query_grad, key_grad, value_grad


def solution(mesh):
    fine = Mesh(mesh.devices.reshape(2, 4, 8, 4, 2), PB + KA)
    split = P(KA + PB, None)
    in_specs = (P(PB, None), split, split, P(PB, None), P(PB, KA))
    out_specs = (P(PB, KA), P(PB, KA), split, split)

    return jax.shard_map(
        per_device, mesh=fine, in_specs=in_specs, out_specs=out_specs, check_vma=False
    )
```

```python
import math

import jax
import jax.numpy as jnp
from jax import lax
from jax.experimental import pallas as pl
from jax.experimental.pallas import tpu as pltpu
from jax.sharding import Mesh, PartitionSpec as P


BLOCK = 128
CHUNK = 512
SCORE_ROWS = 1024
GRAD_ROWS = 1024
DEAD = 1.0e30
F32 = jnp.float32
BF16 = jnp.bfloat16


def nt_dot(a, b):
    return lax.dot_general(a, b, (((1,), (1,)), ((), ())), preferred_element_type=F32)


def identity(size):
    rows = lax.broadcasted_iota(jnp.int32, (size, size), 0)
    cols = lax.broadcasted_iota(jnp.int32, (size, size), 1)
    return (rows == cols).astype(F32).astype(BF16)


def forward_kernel(
    mask_hbm, kv_ref, q_hbm, dout_hbm, weights_ref, out_ref, copies_ref, peak_ref, q_ref, dout_ref,
    stats_ref, scores_a, scores_b, wide, mask_ref, sems,
):
    keys, width = kv_ref.shape[0], kv_ref.shape[1] // 2
    queries, heads = q_ref.shape[0], q_ref.shape[1] // width
    scale = 1.0 / math.sqrt(width)
    loads = [
        pltpu.make_async_copy(mask_hbm, mask_ref, sems.at[0]),
        pltpu.make_async_copy(q_hbm.at[:, :width], q_ref.at[:, :width], sems.at[1]),
        pltpu.make_async_copy(q_hbm.at[:, width:], q_ref.at[:, width:], sems.at[2]),
        pltpu.make_async_copy(dout_hbm, dout_ref, sems.at[3]),
    ]
    for load in loads:
        load.start()
    eye = identity(width)
    wide[width:, :] = jnp.ones((wide.shape[0] - width, keys), BF16)
    for start in range(0, keys, CHUNK):
        rows = slice(start, start + CHUNK)
        wide[:width, rows] = nt_dot(eye, kv_ref[rows, width:]).astype(BF16)
    loads[0].wait()
    loads[1].wait()
    dead = [jnp.where(mask_ref[0, j] > 0, 0.0, DEAD) for j in range(keys // BLOCK)]
    scores = (scores_a, scores_b)
    tops = {}

    def score(h, start):
        query = q_ref[:, h * width : (h + 1) * width]
        block = nt_dot(kv_ref[start : start + SCORE_ROWS, :width], query) * scale
        scores[h % 2][start : start + SCORE_ROWS, :] = block
        for part in range(0, SCORE_ROWS, BLOCK):
            top = jnp.max(block[part : part + BLOCK].reshape(BLOCK // 8, 8, queries), axis=0)
            top = top - dead[(start + part) // BLOCK]
            tops[h] = jnp.maximum(tops[h], top) if h in tops else top

    def weigh(h, j, peak):
        rows = slice(j * BLOCK, (j + 1) * BLOCK)
        block = jnp.exp(scores[h % 2][rows, :] - (peak + dead[j]))
        weights_ref[rows, h * queries : (h + 1) * queries] = block.astype(BF16)

    def combine(h, peak):
        lanes = slice(h * queries, (h + 1) * queries)
        acc = jnp.dot(wide[...], weights_ref[:, lanes], preferred_element_type=F32)
        total = acc[width : width + 1]
        out = acc[:width] / total
        out_ref[h] = out.astype(BF16)
        cotangent = nt_dot(eye, dout_ref[:, h * width : (h + 1) * width])
        stats_ref[h : h + 1, :] = peak + jnp.log(total)
        stats_ref[heads + h : heads + h + 1, :] = jnp.sum(cotangent * out, axis=0, keepdims=True)
        peak_ref[h : h + 1, :] = peak

    for start in range(0, keys, SCORE_ROWS):
        score(0, start)
    loads[2].wait()
    before = None
    for h in range(heads):
        peak = jnp.max(tops[h], axis=0, keepdims=True)
        for start in range(0, keys, SCORE_ROWS):
            if h + 1 < heads:
                score(h + 1, start)
            for j in range(start // BLOCK, (start + SCORE_ROWS) // BLOCK):
                weigh(h, j, peak)
        if before is not None:
            if h == 1:
                loads[3].wait()
            combine(h - 1, before)
        before = peak
    combine(heads - 1, before)
    for n in range(copies_ref.shape[0]):
        copies_ref[n] = stats_ref[...]


def row_mix(stats_ref, heads):
    panels = stats_ref.shape[0]
    top = stats_ref[0, :heads]
    for n in range(1, panels):
        top = jnp.maximum(top, stats_ref[n, :heads])
    total = jnp.zeros_like(top)
    delta = jnp.zeros_like(top)
    for n in range(panels):
        share = jnp.exp(stats_ref[n, :heads] - top)
        total = total + share
        delta = delta + share * stats_ref[n, heads:]
    return top + jnp.log(total), delta / total


def backward_kernel(
    stats_ref, peak_ref, own_ref, kv_ref, q_ref, dout_ref, weights_ref, out_ref,
    keep_ref, send_ref, dkv_ref, dscores, keys_t, mixed_q, mixed_dout, factors, blended,
):
    keys, width = kv_ref.shape[0], kv_ref.shape[1] // 2
    queries, heads = q_ref.shape[0], q_ref.shape[1] // width
    scale = 1.0 / math.sqrt(width)
    core = lax.axis_index("core")
    eye = identity(width)
    for start in range(0, keys, CHUNK):
        rows = slice(start, start + CHUNK)
        keys_t[:, rows] = nt_dot(eye, kv_ref[rows, :width]).astype(BF16)
    row_lse, row_delta = row_mix(stats_ref, heads)
    factor = jnp.exp(peak_ref[...] - row_lse)
    factors[:heads, :] = factor
    factors[heads : 2 * heads, :] = row_delta
    factors[2 * heads :, :] = jnp.exp(own_ref[0, :heads] - row_lse)
    columns = factor.T

    def mix(h):
        rows = slice(h * queries, (h + 1) * queries)
        cols = slice(h * width, (h + 1) * width)
        column = columns[:, h : h + 1]
        mixed_q[rows, :] = (q_ref[:, cols].astype(F32) * column).astype(BF16)
        mixed_dout[rows, :] = (dout_ref[:, cols].astype(F32) * column).astype(BF16)

    def differ(h, start):
        rows = slice(start, start + CHUNK)
        lanes = slice(h * queries, (h + 1) * queries)
        dprobs = nt_dot(kv_ref[rows, width:], dout_ref[:, h * width : (h + 1) * width])
        delta = factors[heads + h : heads + h + 1, :]
        dscores[rows, lanes] = (weights_ref[rows, lanes].astype(F32) * (dprobs - delta)).astype(BF16)

    def project(h):
        lanes = slice(h * queries, (h + 1) * queries)
        acc = jnp.dot(keys_t[...], dscores[:, lanes], preferred_element_type=F32)
        blended[h, :width, :] = (acc * (factors[h : h + 1, :] * scale)).astype(BF16)
        part = out_ref[h].astype(F32) * factors[2 * heads + h : 2 * heads + h + 1, :]
        blended[h, width:, :] = part.astype(BF16)

    for h in range(heads):
        for start in range(0, keys, CHUNK):
            differ(h, start)
        mix(h)
        if h:
            project(h - 1)
    project(heads - 1)

    def one_chunk(index, carry):
        rows = pl.ds(pl.multiple_of(index * GRAD_ROWS, GRAD_ROWS), GRAD_ROWS)
        key_part = jnp.dot(dscores[rows, :], mixed_q[...], preferred_element_type=F32)
        value_part = jnp.dot(weights_ref[rows, :], mixed_dout[...], preferred_element_type=F32)
        dkv_ref[rows, :width] = (key_part * scale).astype(BF16)
        dkv_ref[rows, width:] = value_part.astype(BF16)
        return carry

    lax.fori_loop(0, keys // GRAD_ROWS, one_chunk, 0)
    for index in range(heads // 2):
        keep_ref[index] = blended[2 * index + core]
        send_ref[index] = blended[2 * index + 1 - core]


def pair_kernel(keep_ref, got_ref, own_ref, one_ref, two_ref, three_ref):
    count = keep_ref.shape[0]
    place = lax.axis_index("y_hi")
    own_ref[...] = keep_ref[place].astype(F32) + got_ref[place].astype(F32)
    for step, target in enumerate((one_ref, two_ref, three_ref)):
        spot = lax.rem(place + step + 1, count)
        target[...] = (keep_ref[spot].astype(F32) + got_ref[spot].astype(F32)).astype(BF16)


def rows_kernel(own_ref, one_ref, two_ref, three_ref, query_grad_ref, attended_ref):
    width = query_grad_ref.shape[1]
    total = own_ref[...] + one_ref[...].astype(F32)
    total = total + two_ref[...].astype(F32) + three_ref[...].astype(F32)
    query_grad_ref[...] = total[:width].T
    attended_ref[...] = total[width:].T.astype(BF16)


def shards_kernel(parts_ref, key_grad_ref, value_grad_ref):
    width = key_grad_ref.shape[1]
    both = parts_ref[0].astype(F32)
    for n in range(1, parts_ref.shape[0]):
        both = both + parts_ref[n].astype(F32)
    key_grad_ref[...] = both[:, :width]
    value_grad_ref[...] = both[:, width:]


VMEM = pl.BlockSpec(memory_space=pltpu.VMEM)
FAR = pl.BlockSpec(memory_space=pltpu.HBM)


PB = ("y_lo", "x", "z")
KA = ("y_hi", "core")


def limit(mib):
    return pltpu.CompilerParams(vmem_limit_bytes=mib << 20)


def spread(block, axis):
    size = lax.axis_size(axis)
    copies = jnp.broadcast_to(block[None], (size,) + block.shape)
    return lax.all_to_all(copies, axis, 0, 0, tiled=True).reshape(-1, block.shape[1])


def per_device(queries, keys, values, dout, block_mask):
    rows, row_width = queries.shape
    shard, width = keys.shape
    heads = row_width // width
    pb, high = lax.axis_size(PB), lax.axis_size("y_hi")
    panel = shard * pb
    all_rows = heads * rows
    shape = jax.ShapeDtypeStruct

    kv = spread(jnp.concatenate([keys, values], axis=1), "z")
    kv = spread(kv, ("y_lo", "x"))

    weights, out_parts, stats, peak, q_near, dout_near = pl.pallas_call(
        forward_kernel,
        out_shape=(
            shape((panel, all_rows), BF16),
            shape((heads, width, rows), BF16),
            shape((lax.axis_size(KA), 2 * heads, rows), F32),
            shape((heads, rows), F32),
            shape((rows, row_width), BF16),
            shape((rows, row_width), BF16),
        ),
        in_specs=[FAR, VMEM, FAR, FAR],
        out_specs=(VMEM,) * 6,
        scratch_shapes=[
            pltpu.VMEM((2 * heads, rows), F32),
            pltpu.VMEM((panel, rows), F32),
            pltpu.VMEM((panel, rows), F32),
            pltpu.VMEM((width + 16, panel), BF16),
            pltpu.SMEM(block_mask.shape, jnp.int32),
            pltpu.SemaphoreType.DMA((4,)),
        ],
        compiler_params=limit(20),
        name="forward",
    )(
        *(
            x if x is kv else pltpu.with_memory_space_constraint(x, pltpu.HBM)
            for x in (block_mask, kv, queries, dout)
        )
    )

    all_stats = lax.all_to_all(stats, KA, 0, 0, tiled=True)

    keep, send, dkv = pl.pallas_call(
        backward_kernel,
        out_shape=(
            shape((high, 2 * width, rows), BF16),
            shape((high, 2 * width, rows), BF16),
            shape((panel, 2 * width), BF16),
        ),
        in_specs=[VMEM] * 8,
        out_specs=(VMEM,) * 3,
        scratch_shapes=[
            pltpu.VMEM((panel, all_rows), BF16),
            pltpu.VMEM((width, panel), BF16),
            pltpu.VMEM((all_rows, width), BF16),
            pltpu.VMEM((all_rows, width), BF16),
            pltpu.VMEM((3 * heads, rows), F32),
            pltpu.VMEM((heads, 2 * width, rows), BF16),
        ],
        compiler_params=limit(30),
        name="backward",
    )(all_stats, peak, stats, kv, q_near, dout_near, weights, out_parts)

    dkv_own = lax.all_to_all(dkv.reshape(pb, shard, 2 * width), PB, 0, 0, tiled=True)
    got = lax.ppermute(send, "core", [(0, 1), (1, 0)])
    own, *moves = pl.pallas_call(
        pair_kernel,
        out_shape=(shape((2 * width, rows), F32),) + (shape((2 * width, rows), BF16),) * 3,
        in_specs=[VMEM, VMEM],
        out_specs=(VMEM,) * 4,
        compiler_params=limit(8),
        name="pair",
    )(keep, got)
    moved = [
        lax.ppermute(move, "y_hi", [(i, (i + step + 1) % high) for i in range(high)])
        for step, move in enumerate(moves)
    ]
    query_grad, attended = pl.pallas_call(
        rows_kernel,
        out_shape=(shape((rows, width), F32), shape((rows, width), BF16)),
        in_specs=[VMEM] * 4,
        out_specs=(VMEM,) * 2,
        compiler_params=limit(8),
        name="rows",
    )(own, *moved)
    key_grad, value_grad = pl.pallas_call(
        shards_kernel,
        out_shape=(shape((shard, width), F32), shape((shard, width), F32)),
        in_specs=[VMEM],
        out_specs=(VMEM,) * 2,
        compiler_params=limit(8),
        name="shards",
    )(dkv_own)
    return attended, query_grad, key_grad, value_grad


def solution(mesh):
    fine = Mesh(mesh.devices.reshape(2, 4, 8, 4, 2), PB + KA)
    split = P(KA + PB, None)
    in_specs = (P(PB, None), split, split, P(PB, None), P(PB, KA))
    out_specs = (P(PB, KA), P(PB, KA), split, split)

    return jax.shard_map(
        per_device, mesh=fine, in_specs=in_specs, out_specs=out_specs, check_vma=False
    )
```
